512 devices in a mesh: ev: 8 (over y, x_hi), gx: 16 (over z), gy: 4 (over x_lo, core).
Axes of the slice: x: 4 (x_hi: 2, x_lo: 2; x = x_hi * 2 + x_lo), y: 4, z: 16, core: 2. Of those that a mesh axis runs over, the one named last changes fastest.
Arguments:
- forward_state: float32 [8, 9, 4, 256, 512], P('ev', None, None, 'gx', 'gy'), may hold values from -6 to 6
- adjoint_state: float32 [8, 9, 4, 256, 512], P('ev', None, None, 'gx', 'gy'), may hold values from -6 to 6
- first_lame_parameter: float32 [4, 256, 512], P(None, 'gx', 'gy'), may hold values from 0.5 to 2
- shear_stiffness: float32 [4, 256, 512], P(None, 'gx', 'gy'), may hold values from 0.5 to 1.5
- buoyancy: float32 [4, 256, 512], P(None, 'gx', 'gy'), may hold values from 0.5 to 1.5
- layer_mask: int32 [4, 256, 512], P(None, 'gx', 'gy'), may hold values 0 or 1
- layer_element: int32 [4, 256, 512], P(None, 'gx', 'gy'), may hold values from 0 to 511
- layer_forces: float32 [8, 3, 512], P('ev'), may hold values from -24 to 24
Outputs:
- forward_next: float32 [8, 9, 4, 256, 512], P('ev', None, None, 'gx', 'gy')
- kernels: float32 [3, 4, 256, 512], P(None, None, 'gx', 'gy')
The draws below stay inside these ranges and needn't reach their ends.
All inputs are finite; a program needn't handle non-finite values. No bound on the sum of `layer_mask` on one device may be relied on, other than what follows from the above.
Results may differ from the reference program's by a relative error of at most 0.00002.
Values sent between devices are 32-bit elements; how exact they have to be, the bound alone decides.
No kernel may reach another device: no remote copies, remote signals or barrier semaphores. Data moves between devices by JAX's collectives and lax.ppermute only.
A program may use at most 64 MiB of HBM per device.

```python
import math
import jax
import jax.numpy as jnp
from jax import lax

Z = 4
NELEM = 512
EVENTS = 8
NX = 256
NY = 512


def draw_wavefield(key, salt):
    inner_key = jax.random.fold_in(key, salt)
    shape = (EVENTS, 9, Z, NX, NY)
    values = jnp.clip(jax.random.normal(inner_key, shape, jnp.float32), -6.0, 6.0)
    factor = jnp.where(jnp.arange(9) < 3, 0.1, 1.0).astype(jnp.float32)
    return values * factor[None, :, None, None, None]


def draw_forward_state(key, part):
    return draw_wavefield(key, 11)


def draw_adjoint_state(key, part):
    return draw_wavefield(key, 23)


def touch_ends(values, key, least, high):
    index_at = [jax.random.randint(jax.random.fold_in(key, axis), (), 0, length) for axis, length in enumerate(values.shape)]
    longest = values.shape.index(max(values.shape))
    next_to = index_at[:longest] + [(index_at[longest] + 1) % values.shape[longest]] + index_at[longest + 1:]
    return values.at[tuple(index_at)].set(least).at[tuple(next_to)].set(high)


def level_of(stream_key, dims, split, smallest, high):
    gain = 1.0
    for dim, parts in split:
        draws = jax.random.uniform(jax.random.fold_in(jax.random.fold_in(stream_key, 6), dim), (parts,), jnp.float32, smallest / len(split), high / len(split))
        gain = gain * jnp.repeat(jnp.exp(draws), dims[dim] // parts).reshape((-1,) + (1,) * (len(dims) - 1 - dim))
    return gain


def noise(key, dims, deviation, reach, shards=(), held_as=jnp.bfloat16):
    level = level_of(key, dims, shards, -0.22, 0.18) if shards else 1.0
    drawn = jax.random.normal(key, dims, jnp.float32) * deviation * level
    return jnp.minimum(jnp.maximum(drawn, -reach), reach).astype(held_as)


def setup_inputs(seed: int = 0) -> dict:
    streams_of = jax.random.split(jax.random.key(seed), 9)
    return {
        "forward_state": draw_forward_state(jax.random.fold_in(streams_of[8], 71), 0),
        "adjoint_state": draw_adjoint_state(jax.random.fold_in(streams_of[8], 71), 0),
        "first_lame_parameter": jnp.clip(jnp.exp(math.log(2.0) - 1.3862944 * jax.random.uniform(streams_of[2], (Z, NX, NY), jnp.float32) ** level_of(streams_of[2], (Z, NX, NY), ((1, 16), (2, 4)), -0.2, 0.2)), 0.5, 2.0),
        "shear_stiffness": jnp.clip(jnp.exp(math.log(1.5) - 1.0986123 * jax.random.uniform(streams_of[3], (Z, NX, NY), jnp.float32) ** level_of(streams_of[3], (Z, NX, NY), ((1, 16), (2, 4)), -0.2, 0.2)), 0.5, 1.5),
        "buoyancy": jnp.clip(jnp.exp(math.log(1.5) - 1.0986123 * jax.random.uniform(streams_of[4], (Z, NX, NY), jnp.float32) ** level_of(streams_of[4], (Z, NX, NY), ((1, 16), (2, 4)), -0.2, 0.2)), 0.5, 1.5),
        "layer_mask": touch_ends((jax.random.randint(streams_of[5], (Z, NX, NY), 0, 2) < 1).astype(jnp.int32), jax.random.fold_in(streams_of[5], 1), 0, 1),
        "layer_element": touch_ends(jax.random.randint(streams_of[6], (Z, NX, NY), 0, NELEM), jax.random.fold_in(streams_of[6], 1), 0, NELEM - 1).astype(jnp.int32),
        "layer_forces": noise(streams_of[7], (EVENTS, 3, NELEM), 4.0, 24.0, ((0, 8),), jnp.float32),
    }


inner_coeff = 9.0 / 8.0
outer_coeff = -1.0 / 24.0
advance_time_step = 0.15
axis_of = (1, 2, 0)


def stress_slot(first, second):
    if first == second:
        return first
    return {(0, 1): 3, (1, 0): 3, (0, 2): 4, (2, 0): 4, (1, 2): 5, (2, 1): 5}[(first, second)]


def window(padded, direction, offset):
    starts = [2, 2, 2]
    starts[direction] = 2 + offset
    limits = [starts[dimension] + padded.shape[dimension] - 4 for dimension in range(3)]
    return lax.slice(padded, starts, limits)


def ahead_diff(padded, direction):
    return inner_coeff * (window(padded, direction, 1) - window(padded, direction, 0)) + outer_coeff * (window(padded, direction, 2) - window(padded, direction, -1))


def behind_diff(padded, direction):
    return inner_coeff * (window(padded, direction, 0) - window(padded, direction, -1)) + outer_coeff * (window(padded, direction, 1) - window(padded, direction, -2))


def move_velocity(velocity, padded_stress, buoyancy, forcing, step_now):
    result = []
    for first in range(3):
        pieces = []
        for second in range(3):
            component = padded_stress[stress_slot(first, second)]
            if first == second:
                pieces.append(behind_diff(component, axis_of[second]))
            else:
                pieces.append(ahead_diff(component, axis_of[second]))
        updated = velocity[first] + step_now * (buoyancy * (pieces[0] + pieces[1] + pieces[2]))
        if forcing is not None:
            updated = updated + step_now * forcing[first]
        result.append(updated)
    return jnp.stack(result)


def advance_stress(stress, padded_velocity, first_lame_parameter, shear_stiffness, step_now):
    normal_rates = [ahead_diff(padded_velocity[first], axis_of[first]) for first in range(3)]
    dilatation = normal_rates[0] + normal_rates[1] + normal_rates[2]
    updated = [stress[first] + step_now * (first_lame_parameter * dilatation + 2.0 * shear_stiffness * normal_rates[first]) for first in range(3)]
    shears = []
    for first, second in ((0, 1), (0, 2), (1, 2)):
        shear_rate = behind_diff(padded_velocity[first], axis_of[second]) + behind_diff(padded_velocity[second], axis_of[first])
        updated.append(stress[3 + len(shears)] + step_now * shear_stiffness * shear_rate)
        shears.append(shear_rate)
    return jnp.stack(updated), normal_rates, dilatation, shears


def imaging_condition(forward_pieces_list, adjoint_pieces_list, forward_velocity_field, adjoint_velocity_field, adjoint_before):
    forward_strain_rates, forward_divergence, forward_shear_terms = forward_pieces_list
    adjoint_strain_rates, adjoint_divergence, adjoint_shear_terms = adjoint_pieces_list
    lambda_sensitivity = forward_divergence * adjoint_divergence
    modulus_term = 2.0 * (forward_strain_rates[0] * adjoint_strain_rates[0] + forward_strain_rates[1] * adjoint_strain_rates[1] + forward_strain_rates[2] * adjoint_strain_rates[2])
    modulus_term = modulus_term + forward_shear_terms[0] * adjoint_shear_terms[0] + forward_shear_terms[1] * adjoint_shear_terms[1] + forward_shear_terms[2] * adjoint_shear_terms[2]
    density_term = forward_velocity_field[0] * (adjoint_velocity_field[0] - adjoint_before[0]) + forward_velocity_field[1] * (adjoint_velocity_field[1] - adjoint_before[1]) + forward_velocity_field[2] * (adjoint_velocity_field[2] - adjoint_before[2])
    return jnp.stack([lambda_sensitivity, modulus_term, density_term / advance_time_step])


def pad_every_field(values):
    return jnp.pad(values, ((0, 0), (2, 2), (2, 2), (2, 2)))


def reference(forward_state, adjoint_state, first_lame_parameter, shear_stiffness, buoyancy, layer_mask, layer_element, layer_forces):
    mask_float = layer_mask.astype(jnp.float32)
    outputs = []
    kernels = jnp.zeros((3,) + first_lame_parameter.shape, jnp.float32)
    for member in range(EVENTS):
        forward_wavefield = forward_state[member]
        adjoint_wavefield = adjoint_state[member]
        forcing = jnp.stack([mask_float * jnp.take(layer_forces[member, first], layer_element) for first in range(3)])
        forward_velocity_field = move_velocity(forward_wavefield[:3], pad_every_field(forward_wavefield[3:]), buoyancy, forcing, advance_time_step)
        adjoint_velocity_field = move_velocity(adjoint_wavefield[:3], pad_every_field(adjoint_wavefield[3:]), buoyancy, None, -advance_time_step)
        forward_stress_field, forward_strain_rates, forward_divergence, forward_shear_terms = advance_stress(forward_wavefield[3:], pad_every_field(forward_velocity_field), first_lame_parameter, shear_stiffness, advance_time_step)
        adjoint_stress_field, adjoint_strain_rates, adjoint_divergence, adjoint_shear_terms = advance_stress(adjoint_wavefield[3:], pad_every_field(adjoint_velocity_field), first_lame_parameter, shear_stiffness, -advance_time_step)
        sensitivity_terms = imaging_condition((forward_strain_rates, forward_divergence, forward_shear_terms), (adjoint_strain_rates, adjoint_divergence, adjoint_shear_terms), forward_velocity_field, adjoint_velocity_field, adjoint_wavefield[:3])
        kernels = kernels + sensitivity_terms
        outputs.append(jnp.concatenate([forward_velocity_field, forward_stress_field], 0))
    return jnp.stack(outputs), kernels
```

```python
import jax
import jax.numpy as jnp
from jax import lax
from jax.experimental import pallas as pl
from jax.experimental.pallas import tpu as pltpu
from jax.sharding import PartitionSpec as P

inner_coeff = 9.0 / 8.0
outer_coeff = -1.0 / 24.0
advance_time_step = 0.15
axis_of = (1, 2, 0)


def extended(array, sides, width):
    for axis, dim in sides:
        devices, length = (lax.axis_size(axis), array.shape[dim])
        up = [(i, (i + 1) % devices) for i in range(devices - 1)]
        down = [(j, i) for i, j in up]
        last = lax.slice_in_dim(array, length - width, length, axis=dim)
        first = lax.slice_in_dim(array, 0, width, axis=dim)
        before = lax.ppermute(last, axis, up)
        after = lax.ppermute(first, axis, down)
        array = jnp.concatenate([before, array, after], axis=dim)
    return array


def stress_slot(first, second):
    if first == second:
        return first
    return {(0, 1): 3, (1, 0): 3, (0, 2): 4, (2, 0): 4, (1, 2): 5, (2, 1): 5}[first, second]


def window(padded, direction, offset):
    starts = [2, 2, 2]
    starts[direction] = 2 + offset
    limits = [starts[dimension] + padded.shape[dimension] - 4 for dimension in range(3)]
    return lax.slice(padded, starts, limits)


def ahead_diff(padded, direction):
    return inner_coeff * (
        window(padded, direction, 1) - window(padded, direction, 0)
    ) + outer_coeff * (window(padded, direction, 2) - window(padded, direction, -1))


def behind_diff(padded, direction):
    return inner_coeff * (
        window(padded, direction, 0) - window(padded, direction, -1)
    ) + outer_coeff * (window(padded, direction, 1) - window(padded, direction, -2))


def move_velocity(velocity, padded_stress, buoyancy, forcing, step_now):
    result = []
    for first in range(3):
        pieces = []
        for second in range(3):
            component = padded_stress[stress_slot(first, second)]
            if first == second:
                pieces.append(behind_diff(component, axis_of[second]))
            else:
                pieces.append(ahead_diff(component, axis_of[second]))
        updated = velocity[first] + step_now * (buoyancy * (pieces[0] + pieces[1] + pieces[2]))
        if forcing is not None:
            updated = updated + step_now * forcing[first]
        result.append(updated)
    return jnp.stack(result)


def advance_stress(stress, padded_velocity, first_lame_parameter, shear_stiffness, step_now):
    normal_rates = [ahead_diff(padded_velocity[first], axis_of[first]) for first in range(3)]
    dilatation = normal_rates[0] + normal_rates[1] + normal_rates[2]
    updated = [
        stress[first]
        + step_now
        * (first_lame_parameter * dilatation + 2.0 * shear_stiffness * normal_rates[first])
        for first in range(3)
    ]
    shears = []
    for first, second in ((0, 1), (0, 2), (1, 2)):
        shear_rate = behind_diff(padded_velocity[first], axis_of[second]) + behind_diff(
            padded_velocity[second], axis_of[first]
        )
        updated.append(stress[3 + len(shears)] + step_now * shear_stiffness * shear_rate)
        shears.append(shear_rate)
    return (jnp.stack(updated), normal_rates, dilatation, shears)


def imaging_condition(
    forward_pieces_list,
    adjoint_pieces_list,
    forward_velocity_field,
    adjoint_velocity_field,
    adjoint_before,
):
    forward_strain_rates, forward_divergence, forward_shear_terms = forward_pieces_list
    adjoint_strain_rates, adjoint_divergence, adjoint_shear_terms = adjoint_pieces_list
    lambda_sensitivity = forward_divergence * adjoint_divergence
    modulus_term = 2.0 * (
        forward_strain_rates[0] * adjoint_strain_rates[0]
        + forward_strain_rates[1] * adjoint_strain_rates[1]
        + forward_strain_rates[2] * adjoint_strain_rates[2]
    )
    modulus_term = (
        modulus_term
        + forward_shear_terms[0] * adjoint_shear_terms[0]
        + forward_shear_terms[1] * adjoint_shear_terms[1]
        + forward_shear_terms[2] * adjoint_shear_terms[2]
    )
    density_term = (
        forward_velocity_field[0] * (adjoint_velocity_field[0] - adjoint_before[0])
        + forward_velocity_field[1] * (adjoint_velocity_field[1] - adjoint_before[1])
        + forward_velocity_field[2] * (adjoint_velocity_field[2] - adjoint_before[2])
    )
    return jnp.stack([lambda_sensitivity, modulus_term, density_term / advance_time_step])


def lookup(mask_ref, element_ref, table_ref, out_ref):
    depth, rows, lanes = element_ref.shape
    for z in range(depth):
        for row in range(0, rows, 8):
            element = element_ref[z, row : row + 8, :]
            weight = mask_ref[z, row : row + 8, :].astype(jnp.float32)
            lane = jnp.bitwise_and(element, 127)
            part = jnp.right_shift(element, 7)
            for first in range(3):
                found = jnp.zeros((8, lanes), jnp.float32)
                for k in range(table_ref.shape[1]):
                    entries = jnp.broadcast_to(table_ref[first, k : k + 1, :], (8, lanes))
                    taken = jnp.take_along_axis(entries, lane, axis=1, mode="promise_in_bounds")
                    found = jnp.where(part == k, taken, found)
                out_ref[first, z, row : row + 8, :] = weight * found


def force_field(layer_mask, layer_element, layer_forces):
    table = layer_forces.reshape(3, -1, 128)
    return pl.pallas_call(
        lookup,
        out_shape=jax.ShapeDtypeStruct((3,) + layer_mask.shape, jnp.float32),
        in_specs=[pl.BlockSpec(memory_space=pltpu.VMEM)] * 3,
        out_specs=pl.BlockSpec(memory_space=pltpu.VMEM),
    )(layer_mask, layer_element, table)


def event_sum(terms):
    events = lax.axis_size("ev")
    flat = terms.reshape(-1, 8, 128)
    sent = jnp.broadcast_to(flat[None], (events,) + flat.shape)
    got = lax.all_to_all(sent, "ev", 0, 0, tiled=True)
    return jnp.sum(got, axis=0).reshape(terms.shape)


def pad_depth(values):
    return jnp.pad(values, ((0, 0), (2, 2), (0, 0), (0, 0)))


def shards(
    forward_state,
    adjoint_state,
    first_lame_parameter,
    shear_stiffness,
    buoyancy,
    layer_mask,
    layer_element,
    layer_forces,
):
    forward_wavefield = forward_state[0]
    adjoint_wavefield = adjoint_state[0]
    forcing = force_field(layer_mask, layer_element, layer_forces)
    both_stresses = extended(
        jnp.concatenate([forward_wavefield[3:], adjoint_wavefield[3:]], 0),
        (("gx", 2), ("gy", 3)),
        2,
    )
    forward_padded = pad_depth(both_stresses[:6])
    adjoint_padded = pad_depth(both_stresses[6:])
    forward_velocity_field = move_velocity(
        forward_wavefield[:3], forward_padded, buoyancy, forcing, advance_time_step
    )
    adjoint_velocity_field = move_velocity(
        adjoint_wavefield[:3], adjoint_padded, buoyancy, None, -advance_time_step
    )
    paired_velocity_fields = pad_depth(
        extended(
            jnp.concatenate([forward_velocity_field, adjoint_velocity_field], 0),
            (("gx", 2), ("gy", 3)),
            2,
        )
    )
    forward_velocity_padded = paired_velocity_fields[:3]
    adjoint_velocity_padded = paired_velocity_fields[3:]
    forward_stress_field, forward_strain_rates, forward_divergence, forward_shear_terms = (
        advance_stress(
            forward_wavefield[3:],
            forward_velocity_padded,
            first_lame_parameter,
            shear_stiffness,
            advance_time_step,
        )
    )
    adjoint_stress_field, adjoint_strain_rates, adjoint_divergence, adjoint_shear_terms = (
        advance_stress(
            adjoint_wavefield[3:],
            adjoint_velocity_padded,
            first_lame_parameter,
            shear_stiffness,
            -advance_time_step,
        )
    )
    sensitivity_terms = imaging_condition(
        (forward_strain_rates, forward_divergence, forward_shear_terms),
        (adjoint_strain_rates, adjoint_divergence, adjoint_shear_terms),
        forward_velocity_field,
        adjoint_velocity_field,
        adjoint_wavefield[:3],
    )
    kernels = event_sum(sensitivity_terms)
    forward_next = jnp.concatenate([forward_velocity_field, forward_stress_field], 0)[None]
    return (forward_next, kernels)


def solution(mesh):
    in_specs = (
        P("ev", None, None, "gx", "gy"),
        P("ev", None, None, "gx", "gy"),
        P(None, "gx", "gy"),
        P(None, "gx", "gy"),
        P(None, "gx", "gy"),
        P(None, "gx", "gy"),
        P(None, "gx", "gy"),
        P("ev", None, None),
    )
    out_specs = (P("ev", None, None, "gx", "gy"), P(None, None, "gx", "gy"))
    return jax.shard_map(shards, mesh=mesh, in_specs=in_specs, out_specs=out_specs, check_vma=False)
```

```python
import functools

import jax
import jax.numpy as jnp
from jax import lax
from jax.experimental import pallas as pl
from jax.experimental.pallas import tpu as pltpu
from jax.sharding import PartitionSpec as P

inner_coeff = 9.0 / 8.0
outer_coeff = -1.0 / 24.0
advance_time_step = 0.15
vmem_limit = 16 << 20

VX, VY, VZ, SXX, SYY, SZZ, SXY, SXZ, SYZ = range(9)
ADJOINT = 9
BUOYANCY = 18
FIELDS = 19
SUB, LANE = 8, 128
RING = 24
SLOT = 6
SLOTS = 21


def row_slots(depth):
    three = [
        (base + field, z)
        for z in range(depth)
        for base in (0, ADJOINT)
        for field in (SXX, SXY, SXZ)
    ]
    two = [
        (field, z)
        for z in range(depth)
        for field in range(FIELDS)
        if field == BUOYANCY or field % ADJOINT not in (SXX, SXY, SXZ)
    ]
    slots, tile, sub = [], 0, 0
    while three or two:
        if three and sub <= 3:
            (field, z), rows = three.pop(0), 3
        else:
            (field, z), rows = two.pop(0), 2
        slots.append((field, z, rows, tile, sub))
        sub += rows
        if sub + 2 > SUB:
            tile, sub = tile + 1, 0
    return slots, tile + (sub > 0)


def column_slots(depth):
    return [(field, z) for z in range(depth) for field in range(FIELDS)]


def turn(value, amount, axis):
    amount %= value.shape[axis]
    return pltpu.roll(value, amount, axis) if amount else value


def sublanes():
    return lax.broadcasted_iota(jnp.int32, (SUB, LANE), 0)


def column_slot_of():
    return jnp.bitwise_and(lax.broadcasted_iota(jnp.int32, (SUB, LANE), 1) + 3, LANE - 1)


def even(axis):
    return jnp.bitwise_and(lax.axis_index(axis), 1) == 0


def pick(condition, first, second):
    return jnp.where(jnp.broadcast_to(condition, first.shape), first, second)


def lookup(mask_ref, element_ref, table_ref, z, row):
    element = element_ref[z, row : row + SUB, :]
    weight = mask_ref[z, row : row + SUB, :].astype(jnp.float32)
    lane = jnp.bitwise_and(element, LANE - 1)
    part = jnp.right_shift(element, 7)
    parts = table_ref.shape[2] // LANE
    found = []
    for first in range(3):
        value = None
        for k in range(parts):
            part_lanes = slice(LANE * k, LANE * (k + 1))
            entries = jnp.broadcast_to(table_ref[first, :, part_lanes], (SUB, LANE))
            taken = jnp.take_along_axis(entries, lane, axis=1, mode="promise_in_bounds")
            value = taken if k == 0 else jnp.where(part == k, taken, value)
        found.append(weight * value)
    return found


def pack_columns(load, depth, write):
    slot = column_slot_of()
    value = None
    slots = column_slots(depth)
    for k, (field, z) in enumerate(slots):
        tile, place = divmod(k, SLOTS)
        moved = turn(load(field, z), SLOT * place, 1)
        if place == 0:
            value = moved
        else:
            value = jnp.where(slot >= SLOT * place, moved, value)
        if place == SLOTS - 1 or k == len(slots) - 1:
            write(tile, value)


def first_pack(
    forward_hbm,
    adjoint_hbm,
    buoyancy_hbm,
    mask_hbm,
    element_hbm,
    table_hbm,
    first_ref,
    second_ref,
    columns_ref,
    pushed_ref,
    forward_ref,
    adjoint_ref,
    buoyancy_ref,
    mask_ref,
    element_ref,
    table_ref,
    arrivals,
):
    depth, rows, _ = buoyancy_ref.shape
    loads = [
        pltpu.make_async_copy(source, target, arrivals.at[k])
        for k, (source, target) in enumerate(
            (
                (element_hbm, element_ref),
                (mask_hbm, mask_ref),
                (table_hbm, table_ref),
                (forward_hbm, forward_ref),
                (buoyancy_hbm, buoyancy_ref),
                (adjoint_hbm, adjoint_ref),
            )
        )
    ]
    for copy in loads:
        copy.start()
    for copy in loads[:4]:
        copy.wait()
    for z in range(depth):
        for row in range(0, rows, SUB):
            forcing = lookup(mask_ref, element_ref, table_ref, z, row)
            for i in range(3):
                velocity = forward_ref[0, i, z, row : row + SUB, :]
                pushed_ref[i, z, row : row + SUB, :] = velocity + advance_time_step * forcing[i]
    for copy in loads[4:]:
        copy.wait()

    def load(field, z, row):
        if field == BUOYANCY:
            return buoyancy_ref[z, row : row + SUB, :]
        if field >= ADJOINT:
            return adjoint_ref[0, field - ADJOINT, z, row : row + SUB, :]
        if field < 3:
            return pushed_ref[field, z, row : row + SUB, :]
        return forward_ref[0, field, z, row : row + SUB, :]

    slots, tiles = row_slots(depth)
    sub = sublanes()
    is_even = even("gx")
    for tile in range(tiles):
        up, down = None, None
        for field, z, count, at, start in slots:
            if at != tile:
                continue
            last = turn(load(field, z, rows - SUB), start + count, 0)
            first = turn(load(field, z, 0), start, 0)
            up = last if up is None else jnp.where(sub >= start, last, up)
            down = first if down is None else jnp.where(sub >= start, first, down)
        first_ref[tile] = pick(is_even, up, down)
        second_ref[tile] = pick(is_even, down, up)

    for row in range(0, rows, SUB):

        def write(tile, value, row=row):
            columns_ref[tile, row : row + SUB, :] = value

        pack_columns(lambda field, z, row=row: load(field, z, row), depth, write)


def second_pack(first_ref, second_ref, own_ref, columns_ref, rows_ref):
    depth = rows_ref.shape[1]
    slots, _ = row_slots(depth)
    is_even = even("gx")
    sub = sublanes()
    tiles = {}
    for field, z, count, tile, start in slots:
        if tile not in tiles:
            first, second = first_ref[tile], second_ref[tile]
            tiles[tile] = (pick(is_even, second, first), pick(is_even, first, second))
        up, down = tiles[tile]
        before = turn(up, SUB - count - start, 0)
        after = turn(down, -start, 0)
        rows_ref[field, z] = jnp.where(sub < 4, after, before)
    own = own_ref.shape[1]
    columns_ref[:, :own, :] = own_ref[...]

    def write(tile, value):
        columns_ref[tile, own:, :] = value

    pack_columns(lambda field, z: rows_ref[field, z], depth, write)


def ahead(value, axis):
    return inner_coeff * (turn(value, -1, axis) - value) + outer_coeff * (
        turn(value, -2, axis) - turn(value, 1, axis)
    )


def behind(value, axis):
    return inner_coeff * (value - turn(value, 1, axis)) + outer_coeff * (
        turn(value, -1, axis) - turn(value, 2, axis)
    )


def depth_diff(plane, z, depth, offset):
    inside = lambda k: plane(k) if 0 <= k < depth else None

    def difference(high, low):
        if high is None:
            return None if low is None else -low
        return high if low is None else high - low

    near = difference(inside(z + 1 + offset), inside(z + offset))
    far = difference(inside(z + 2 + offset), inside(z - 1 + offset))
    total = inner_coeff * near
    return total if far is None else total + outer_coeff * far


def advance(
    forward_ref,
    adjoint_ref,
    pushed_ref,
    buoyancy_ref,
    rows_ref,
    first_ref,
    second_ref,
    terms_ref,
    moved_ref,
    rates_ref,
    field_ref,
    speed_ref,
):
    depth, rows, _ = buoyancy_ref.shape
    slot = column_slot_of()
    from_next = slot >= SLOT * SLOTS
    for place in range(SLOTS):
        from_next = from_next | ((slot >= SLOT * place + 3) & (slot < SLOT * place + 6))
    is_even = jnp.broadcast_to(even("gy"), (SUB, LANE))
    from_first = from_next == is_even
    merged = {}
    for k, (field, z) in enumerate(column_slots(depth)):
        if field == BUOYANCY:
            own = buoyancy_ref[z]
        elif field >= ADJOINT:
            own = adjoint_ref[0, field - ADJOINT, z]
        elif field < 3:
            own = pushed_ref[field, z]
        else:
            own = forward_ref[0, field, z]
        field_ref[field, z, :rows, :LANE] = own
        field_ref[field, z, rows:, :LANE] = rows_ref[field, z]
        tile, place = divmod(k, SLOTS)
        for row in range(0, RING, SUB):
            if (tile, row) not in merged:
                merged[tile, row] = jnp.where(
                    from_first,
                    first_ref[tile, row : row + SUB, :],
                    second_ref[tile, row : row + SUB, :],
                )
            field_ref[field, z, row : row + SUB, LANE:] = turn(
                merged[tile, row], -SLOT * place, 1
            )

    for base, step in ((0, advance_time_step), (ADJOINT, -advance_time_step)):
        for z in range(depth):
            get = lambda field: field_ref[base + field, z]
            along = lambda field, offset: depth_diff(
                lambda k: field_ref[base + field, k], z, depth, offset
            )
            scaled = step * field_ref[BUOYANCY, z]
            sxy, sxz, syz = get(SXY), get(SXZ), get(SYZ)
            speed_ref[base // 3, z] = get(VX) + scaled * (
                behind(get(SXX), 0) + ahead(sxy, 1) + along(SXZ, 0)
            )
            speed_ref[base // 3 + 1, z] = get(VY) + scaled * (
                ahead(sxy, 0) + behind(get(SYY), 1) + along(SYZ, 0)
            )
            speed_ref[base // 3 + 2, z] = get(VZ) + scaled * (
                ahead(sxz, 0) + ahead(syz, 1) + along(SZZ, -1)
            )

    for z in range(depth):
        rates = []
        for base in (0, 3):
            wide = lambda i: speed_ref[base + i, z, :rows, :]
            tall = lambda i: speed_ref[base + i, z, :, :LANE]
            along = lambda i, offset: depth_diff(
                lambda k: speed_ref[base + i, k, :rows, :LANE], z, depth, offset
            )
            over_x = lambda i, way: way(tall(i), 0)[:rows]
            over_y = lambda i, way: way(wide(i), 1)[:, :LANE]
            rates.append(
                (
                    over_x(0, ahead),
                    over_y(1, ahead),
                    along(2, 0),
                    over_y(0, behind) + over_x(1, behind),
                    along(0, -1) + over_x(2, behind),
                    along(1, -1) + over_y(2, behind),
                )
            )
        one, two = rates
        dilatation = one[0] + one[1] + one[2]
        other = two[0] + two[1] + two[2]
        for i in range(3):
            moved_ref[i, z] = speed_ref[i, z, :rows, :LANE]
        for i in range(6):
            rates_ref[i, z] = one[i]
        modulus = 2.0 * (one[0] * two[0] + one[1] * two[1] + one[2] * two[2])
        modulus = modulus + one[3] * two[3] + one[4] * two[4] + one[5] * two[5]
        density = sum(
            speed_ref[i, z, :rows, :LANE]
            * (speed_ref[3 + i, z, :rows, :LANE] - adjoint_ref[0, i, z])
            for i in range(3)
        )
        density = density / advance_time_step
        for copy in range(terms_ref.shape[0]):
            terms_ref[copy, 0, z] = dilatation * other
            terms_ref[copy, 1, z] = modulus
            terms_ref[copy, 2, z] = density


def advance_stress(forward_ref, lame_ref, shear_ref, moved_ref, rates_ref, next_ref):
    for z in range(lame_ref.shape[0]):
        shear = shear_ref[z]
        lame = lame_ref[z]
        dilatation = rates_ref[0, z] + rates_ref[1, z] + rates_ref[2, z]
        for i in range(3):
            next_ref[0, i, z] = moved_ref[i, z]
            next_ref[0, 3 + i, z] = forward_ref[0, 3 + i, z] + advance_time_step * (
                lame * dilatation + 2.0 * shear * rates_ref[i, z]
            )
            next_ref[0, 6 + i, z] = forward_ref[0, 6 + i, z] + advance_time_step * (
                shear * rates_ref[3 + i, z]
            )


def on_chip(kernel, out_shapes, scratch=(), cost=0, held=True):
    vmem = pl.BlockSpec(memory_space=pltpu.VMEM)
    space = pltpu.VMEM if held else pltpu.HBM
    place = lambda value: pltpu.with_memory_space_constraint(value, space)
    return lambda *operands: pl.pallas_call(
        kernel,
        out_shape=[pltpu.VMEM(shape, jnp.float32) for shape in out_shapes],
        in_specs=[vmem if held else pl.BlockSpec(memory_space=pl.ANY)] * len(operands),
        out_specs=[vmem] * len(out_shapes),
        scratch_shapes=list(scratch),
        cost_estimate=pl.CostEstimate(flops=cost, bytes_accessed=cost, transcendentals=0),
        compiler_params=pltpu.CompilerParams(vmem_limit_bytes=vmem_limit),
    )(*map(place, operands))


def swaps(devices, start):
    pairs = [(i, i + 1) for i in range(start, devices - 1, 2)]
    return pairs + [(j, i) for i, j in pairs]


def exchange(first, second, axis):
    devices = lax.axis_size(axis)
    return (
        lax.ppermute(first, axis, swaps(devices, 0)),
        lax.ppermute(second, axis, swaps(devices, 1)),
    )


def shards(
    forward_state,
    adjoint_state,
    first_lame_parameter,
    shear_stiffness,
    buoyancy,
    layer_mask,
    layer_element,
    layer_forces,
):
    depth, rows, lanes = buoyancy.shape
    events = lax.axis_size("ev")
    table = jnp.transpose(layer_forces, (1, 0, 2))
    tiles = row_slots(depth)[1]
    column_tiles = -(-depth * FIELDS // SLOTS)
    message = (tiles, SUB, lanes)
    state, plane = forward_state.shape, buoyancy.shape
    first, second, columns, pushed, forward_here, adjoint_here, buoyancy_here = on_chip(
        first_pack,
        [message, message, (column_tiles, rows, lanes), (3,) + plane, state, state, plane],
        [
            pltpu.VMEM(plane, jnp.int32),
            pltpu.VMEM(plane, jnp.int32),
            pltpu.VMEM(table.shape, jnp.float32),
            pltpu.SemaphoreType.DMA((6,)),
        ],
        cost=2_000_000,
        held=False,
    )(forward_state, adjoint_state, buoyancy, layer_mask, layer_element, table)
    first, second = exchange(first, second, "gx")
    columns, edge_rows = on_chip(
        second_pack,
        [(column_tiles, RING, lanes), (FIELDS, depth, SUB, lanes)],
        cost=1_000_000,
    )(first, second, columns)
    first, second = exchange(columns, columns, "gy")
    terms, moved, rates = on_chip(
        advance,
        [(events, 3) + plane, (3,) + plane, (6,) + plane],
        [
            pltpu.VMEM((FIELDS, depth, RING, 2 * lanes), jnp.float32),
            pltpu.VMEM((6, depth, RING, 2 * lanes), jnp.float32),
        ],
        cost=4_000_000,
    )(forward_here, adjoint_here, pushed, buoyancy_here, edge_rows, first, second)
    (forward_next,) = on_chip(advance_stress, [state], cost=2_000_000)(
        forward_here, first_lame_parameter, shear_stiffness, moved, rates
    )
    kernels = jnp.sum(lax.all_to_all(terms, "ev", 0, 0, tiled=True), axis=0)
    return (forward_next, kernels)


def solution(mesh):
    in_specs = (
        P("ev", None, None, "gx", "gy"),
        P("ev", None, None, "gx", "gy"),
        P(None, "gx", "gy"),
        P(None, "gx", "gy"),
        P(None, "gx", "gy"),
        P(None, "gx", "gy"),
        P(None, "gx", "gy"),
        P("ev", None, None),
    )
    out_specs = (P("ev", None, None, "gx", "gy"), P(None, None, "gx", "gy"))
    return jax.shard_map(shards, mesh=mesh, in_specs=in_specs, out_specs=out_specs, check_vma=False)
```

```python
import functools

import jax
import jax.numpy as jnp
from jax import lax
from jax.experimental import pallas as pl
from jax.experimental.pallas import tpu as pltpu
from jax.sharding import PartitionSpec as P

inner_coeff = 9.0 / 8.0
outer_coeff = -1.0 / 24.0
ratio = outer_coeff / inner_coeff
advance_time_step = 0.15
vmem_limit = 16 << 20

PX, PY, PZ, SXX, SYY, SXY, SXZ, SYZ = range(8)
ADJOINT = 8
BUOYANCY = 16
FIELDS = 17
STATE_SLOT = {SXX: 3, SYY: 4, SXY: 6, SXZ: 7, SYZ: 8}
ALONG_X = (SXX, SXY, SXZ)
SUB, LANE = 8, 128
RING = 24
SLOT = 6
SLOTS = 21


def row_slots(depth):
    three = [
        (base + field, z) for z in range(depth) for base in (0, ADJOINT) for field in ALONG_X
    ]
    two = [
        (field, z)
        for z in range(depth)
        for field in range(FIELDS)
        if field == BUOYANCY or field % ADJOINT not in ALONG_X
    ]
    slots, tile, sub = [], 0, 0
    while three or two:
        if three and sub <= 3:
            (field, z), rows = three.pop(0), 3
        else:
            (field, z), rows = two.pop(0), 2
        slots.append((field, z, rows, tile, sub))
        sub += rows
        if sub + 2 > SUB:
            tile, sub = tile + 1, 0
    return slots, tile + (sub > 0)


def column_slots(depth):
    return [(field, z) for z in range(depth) for field in range(FIELDS)]


def turn(value, amount, axis):
    amount %= value.shape[axis]
    return pltpu.roll(value, amount, axis) if amount else value


def sublanes():
    return lax.broadcasted_iota(jnp.int32, (SUB, LANE), 0)


def column_slot_of():
    return jnp.bitwise_and(lax.broadcasted_iota(jnp.int32, (SUB, LANE), 1) + 3, LANE - 1)


def even(axis):
    return jnp.bitwise_and(lax.axis_index(axis), 1) == 0


def pick(condition, first, second):
    return jnp.where(jnp.broadcast_to(condition, first.shape), first, second)


def lookup(mask_ref, element_ref, table_ref, z, row):
    element = element_ref[z, row : row + SUB, :]
    weight = mask_ref[z, row : row + SUB, :].astype(jnp.float32)
    lane = jnp.bitwise_and(element, LANE - 1)
    part = jnp.right_shift(element, 7)
    parts = table_ref.shape[2] // LANE
    found = []
    for first in range(3):
        value = None
        for k in range(parts):
            part_lanes = slice(LANE * k, LANE * (k + 1))
            entries = jnp.broadcast_to(table_ref[first, :, part_lanes], (SUB, LANE))
            taken = jnp.take_along_axis(entries, lane, axis=1, mode="promise_in_bounds")
            value = taken if k == 0 else jnp.where(part == k, taken, value)
        found.append(weight * value)
    return found


def pack_columns(load, depth, write):
    slot = column_slot_of()
    value = None
    slots = column_slots(depth)
    for k, (field, z) in enumerate(slots):
        tile, place = divmod(k, SLOTS)
        moved = turn(load(field, z), SLOT * place, 1)
        if place == 0:
            value = moved
        else:
            value = jnp.where(slot >= SLOT * place, moved, value)
        if place == SLOTS - 1 or k == len(slots) - 1:
            write(tile, value)


def depth_diff(plane, z, depth, offset):
    inside = lambda k: plane(k) if 0 <= k < depth else None

    def difference(high, low):
        if high is None:
            return None if low is None else -low
        return high if low is None else high - low

    near = difference(inside(z + 1 + offset), inside(z + offset))
    far = difference(inside(z + 2 + offset), inside(z - 1 + offset))
    return near if far is None else near + ratio * far


def own_tile(pushed_ref, forward_ref, adjoint_ref, buoyancy_ref, field, z, row):
    rows = slice(row, row + SUB)
    if field == BUOYANCY:
        return buoyancy_ref[z, rows, :]
    adjoint, field = divmod(field, ADJOINT)
    if field <= PZ:
        return pushed_ref[3 * adjoint + field, z, rows, :]
    return (adjoint_ref if adjoint else forward_ref)[0, STATE_SLOT[field], z, rows, :]


def first_pack(
    forward_hbm,
    adjoint_hbm,
    buoyancy_hbm,
    mask_hbm,
    element_hbm,
    table_hbm,
    first_ref,
    second_ref,
    pushed_ref,
    forward_ref,
    adjoint_ref,
    buoyancy_ref,
    mask_ref,
    element_ref,
    table_ref,
    arrivals,
):
    depth, rows, _ = buoyancy_ref.shape
    loads = [
        pltpu.make_async_copy(source, target, arrivals.at[k])
        for k, (source, target) in enumerate(
            (
                (element_hbm, element_ref),
                (mask_hbm, mask_ref),
                (table_hbm, table_ref),
                (buoyancy_hbm, buoyancy_ref),
                (forward_hbm, forward_ref),
                (adjoint_hbm, adjoint_ref),
            )
        )
    ]
    for copy in loads:
        copy.start()
    for copy in loads[:3]:
        copy.wait()
    cells = [(z, row) for z in range(depth) for row in range(0, rows, SUB)]
    for z, row in cells:
        for i, forcing in enumerate(lookup(mask_ref, element_ref, table_ref, z, row)):
            pushed_ref[i, z, row : row + SUB, :] = advance_time_step * forcing
    loads[3].wait()
    for state_ref, copy, base, step in (
        (forward_ref, loads[4], 0, advance_time_step),
        (adjoint_ref, loads[5], 3, -advance_time_step),
    ):
        copy.wait()
        for z, row in cells:
            part = slice(row, row + SUB)
            scaled = (step * inner_coeff) * buoyancy_ref[z, part, :]
            for i, (field, offset) in enumerate(((7, 0), (8, 0), (5, -1))):
                along = depth_diff(lambda k: state_ref[0, field, k, part, :], z, depth, offset)
                value = state_ref[0, i, z, part, :] + scaled * along
                if base == 0:
                    value = value + pushed_ref[i, z, part, :]
                pushed_ref[base + i, z, part, :] = value

    load = functools.partial(own_tile, pushed_ref, forward_ref, adjoint_ref, buoyancy_ref)
    slots, tiles = row_slots(depth)
    sub = sublanes()
    is_even = even("gx")
    for tile in range(tiles):
        up, down = None, None
        for field, z, count, at, start in slots:
            if at != tile:
                continue
            last = turn(load(field, z, rows - SUB), start + count, 0)
            first = turn(load(field, z, 0), start, 0)
            up = last if up is None else jnp.where(sub >= start, last, up)
            down = first if down is None else jnp.where(sub >= start, first, down)
        first_ref[tile] = pick(is_even, up, down)
        second_ref[tile] = pick(is_even, down, up)


def own_columns(pushed_ref, forward_ref, adjoint_ref, buoyancy_ref, columns_ref):
    depth, rows, _ = buoyancy_ref.shape
    load = functools.partial(own_tile, pushed_ref, forward_ref, adjoint_ref, buoyancy_ref)
    for row in range(0, rows, SUB):

        def write(tile, value, row=row):
            columns_ref[tile, row : row + SUB, :] = value

        pack_columns(lambda field, z, row=row: load(field, z, row), depth, write)


def second_pack(first_ref, second_ref, own_ref, columns_ref, rows_ref):
    depth = rows_ref.shape[1]
    slots, _ = row_slots(depth)
    is_even = even("gx")
    sub = sublanes()
    tiles = {}
    for field, z, count, tile, start in slots:
        if tile not in tiles:
            first, second = first_ref[tile], second_ref[tile]
            tiles[tile] = (pick(is_even, second, first), pick(is_even, first, second))
        up, down = tiles[tile]
        before = turn(up, SUB - count - start, 0)
        after = turn(down, -start, 0)
        rows_ref[field, z] = jnp.where(sub < 4, after, before)
    own = own_ref.shape[1]
    columns_ref[:, :own, :] = own_ref[...]

    def write(tile, value):
        columns_ref[tile, own:, :] = value

    pack_columns(lambda field, z: rows_ref[field, z], depth, write)


def ahead(value, axis):
    return (turn(value, -1, axis) - value) + ratio * (turn(value, -2, axis) - turn(value, 1, axis))


def behind(value, axis):
    return (value - turn(value, 1, axis)) + ratio * (turn(value, -1, axis) - turn(value, 2, axis))


def advance(
    forward_ref,
    adjoint_ref,
    pushed_ref,
    buoyancy_ref,
    rows_ref,
    first_ref,
    second_ref,
    terms_ref,
    moved_ref,
    rates_ref,
    field_ref,
    speed_ref,
):
    depth, rows, _ = buoyancy_ref.shape
    load = functools.partial(own_tile, pushed_ref, forward_ref, adjoint_ref, buoyancy_ref)
    slot = column_slot_of()
    from_next = slot >= SLOT * SLOTS
    for place in range(SLOTS):
        from_next = from_next | ((slot >= SLOT * place + 3) & (slot < SLOT * place + 6))
    from_first = from_next == jnp.broadcast_to(even("gy"), (SUB, LANE))
    merged = {}
    for k, (field, z) in enumerate(column_slots(depth)):
        tile, place = divmod(k, SLOTS)
        for row in range(0, RING, SUB):
            part = slice(row, row + SUB)
            field_ref[field, z, part, :LANE] = (
                load(field, z, row) if row < rows else rows_ref[field, z]
            )
            if (tile, row) not in merged:
                merged[tile, row] = jnp.where(
                    from_first, first_ref[tile, part, :], second_ref[tile, part, :]
                )
            field_ref[field, z, part, LANE:] = turn(merged[tile, row], -SLOT * place, 1)

    for state, step in ((0, advance_time_step), (1, -advance_time_step)):
        for z in range(depth):
            get = lambda field: field_ref[state * ADJOINT + field, z]
            scaled = (step * inner_coeff) * field_ref[BUOYANCY, z]
            sxy = get(SXY)
            changes = (
                behind(get(SXX), 0) + ahead(sxy, 1),
                ahead(sxy, 0) + behind(get(SYY), 1),
                ahead(get(SXZ), 0) + ahead(get(SYZ), 1),
            )
            for i, change in enumerate(changes):
                speed_ref[3 * state + i, z] = get(i) + scaled * change

    for z in range(depth):
        rates = []
        for base in (0, 3):
            along = lambda i, offset: depth_diff(
                lambda k: speed_ref[base + i, k, :rows, :LANE], z, depth, offset
            )
            over_x = lambda i, way: way(speed_ref[base + i, z, :, :LANE], 0)[:rows]
            over_y = lambda i, way: way(speed_ref[base + i, z, :rows, :], 1)[:, :LANE]
            rates.append(
                (
                    over_x(0, ahead),
                    over_y(1, ahead),
                    along(2, 0),
                    over_y(0, behind) + over_x(1, behind),
                    along(0, -1) + over_x(2, behind),
                    along(1, -1) + over_y(2, behind),
                )
            )
        one, two = rates
        first_invariant = (one[0] + one[1] + one[2]) * (two[0] + two[1] + two[2])
        modulus = 2.0 * (one[0] * two[0] + one[1] * two[1] + one[2] * two[2])
        modulus = modulus + one[3] * two[3] + one[4] * two[4] + one[5] * two[5]
        density = None
        for i in range(3):
            moved = speed_ref[i, z, :rows, :LANE]
            moved_ref[i, z] = moved
            gain = moved * (speed_ref[3 + i, z, :rows, :LANE] - adjoint_ref[0, i, z])
            density = gain if density is None else density + gain
        for i in range(6):
            rates_ref[i, z] = one[i]
        terms_ref[0, z] = (inner_coeff * inner_coeff) * first_invariant
        terms_ref[1, z] = (inner_coeff * inner_coeff) * modulus
        terms_ref[2, z] = density / advance_time_step


def advance_stress(
    forward_ref, lame_ref, shear_ref, moved_ref, rates_ref, next_hbm, next_ref, leaves
):
    step = advance_time_step * inner_coeff
    for z in range(lame_ref.shape[0]):
        shear = step * shear_ref[z]
        dilatation = rates_ref[0, z] + rates_ref[1, z] + rates_ref[2, z]
        pressure = step * lame_ref[z] * dilatation
        for i in range(3):
            next_ref[0, i, z] = moved_ref[i, z]
            next_ref[0, 3 + i, z] = forward_ref[0, 3 + i, z] + (
                pressure + 2.0 * shear * rates_ref[i, z]
            )
            next_ref[0, 6 + i, z] = forward_ref[0, 6 + i, z] + shear * rates_ref[3 + i, z]
    copy = pltpu.make_async_copy(next_ref, next_hbm, leaves)
    copy.start()
    copy.wait()


def add_pair(one_ref, two_ref, _, sum_ref):
    total = one_ref[...] + two_ref[...]
    for copy in range(sum_ref.shape[0]):
        sum_ref[copy] = total


def on_chip(kernel, out_shapes, scratch=(), cost=0, far=(), away=()):
    vmem, anywhere = [pl.BlockSpec(memory_space=space) for space in (pltpu.VMEM, pl.ANY)]
    place = lambda k, value: pltpu.with_memory_space_constraint(
        value, pltpu.HBM if k in far else pltpu.VMEM
    )
    return lambda *operands: pl.pallas_call(
        kernel,
        out_shape=[
            (pltpu.HBM if k in away else pltpu.VMEM)(shape, jnp.float32)
            for k, shape in enumerate(out_shapes)
        ],
        in_specs=[anywhere if k in far else vmem for k in range(len(operands))],
        out_specs=[anywhere if k in away else vmem for k in range(len(out_shapes))],
        scratch_shapes=list(scratch),
        cost_estimate=pl.CostEstimate(flops=cost, bytes_accessed=cost, transcendentals=0),
        compiler_params=pltpu.CompilerParams(vmem_limit_bytes=vmem_limit),
    )(*[place(k, value) for k, value in enumerate(operands)])


def swaps(devices, start):
    pairs = [(i, i + 1) for i in range(start, devices - 1, 2)]
    return pairs + [(j, i) for i, j in pairs]


def exchange(first, second, axis):
    devices = lax.axis_size(axis)
    return (
        lax.ppermute(first, axis, swaps(devices, 0)),
        lax.ppermute(second, axis, swaps(devices, 1)),
    )


def shards(
    forward_state,
    adjoint_state,
    first_lame_parameter,
    shear_stiffness,
    buoyancy,
    layer_mask,
    layer_element,
    layer_forces,
):
    depth, rows, lanes = buoyancy.shape
    events = lax.axis_size("ev")
    table = jnp.transpose(layer_forces, (1, 0, 2))
    tiles = row_slots(depth)[1]
    column_tiles = -(-depth * FIELDS // SLOTS)
    message = (tiles, SUB, lanes)
    state, plane = forward_state.shape, buoyancy.shape
    first, second, pushed, forward_here, adjoint_here, buoyancy_here = on_chip(
        first_pack,
        [message, message, (6,) + plane, state, state, plane],
        [
            pltpu.VMEM(plane, jnp.int32),
            pltpu.VMEM(plane, jnp.int32),
            pltpu.VMEM(table.shape, jnp.float32),
            pltpu.SemaphoreType.DMA((6,)),
        ],
        cost=2_000_000,
        far=range(6),
    )(forward_state, adjoint_state, buoyancy, layer_mask, layer_element, table)
    first, second = exchange(first, second, "gx")
    (columns,) = on_chip(own_columns, [(column_tiles, rows, lanes)], cost=1_000_000)(
        pushed, forward_here, adjoint_here, buoyancy_here
    )
    columns, edge_rows = on_chip(
        second_pack,
        [(column_tiles, RING, lanes), (FIELDS, depth, SUB, lanes)],
        cost=1_000_000,
    )(first, second, columns)
    first, second = exchange(columns, columns, "gy")
    terms, moved, rates = on_chip(
        advance,
        [(3,) + plane, (3,) + plane, (6,) + plane],
        [
            pltpu.VMEM((FIELDS, depth, RING, 2 * lanes), jnp.float32),
            pltpu.VMEM((6, depth, RING, 2 * lanes), jnp.float32),
        ],
        cost=4_000_000,
    )(forward_here, adjoint_here, pushed, buoyancy_here, edge_rows, first, second)
    partner = lax.ppermute(terms, "ev", [(i, i ^ 1) for i in range(events)])
    (forward_next,) = on_chip(
        advance_stress,
        [state],
        [pltpu.VMEM(state, jnp.float32), pltpu.SemaphoreType.DMA(())],
        cost=2_000_000,
        away=(0,),
    )(
        forward_here, first_lame_parameter, shear_stiffness, moved, rates
    )
    (pairs,) = on_chip(add_pair, [(events // 2, 3) + plane], cost=500_000, far=(2,))(
        terms, partner, forward_next
    )
    groups = [list(range(k, events, 2)) for k in range(2)]
    kernels = jnp.sum(
        lax.all_to_all(pairs, "ev", 0, 0, axis_index_groups=groups, tiled=True), axis=0
    )
    return (forward_next, kernels)


def solution(mesh):
    in_specs = (
        P("ev", None, None, "gx", "gy"),
        P("ev", None, None, "gx", "gy"),
        P(None, "gx", "gy"),
        P(None, "gx", "gy"),
        P(None, "gx", "gy"),
        P(None, "gx", "gy"),
        P(None, "gx", "gy"),
        P("ev", None, None),
    )
    out_specs = (P("ev", None, None, "gx", "gy"), P(None, None, "gx", "gy"))
    return jax.shard_map(shards, mesh=mesh, in_specs=in_specs, out_specs=out_specs, check_vma=False)
```

```python
import functools

import jax
import jax.numpy as jnp
from jax import lax
from jax.experimental import pallas as pl
from jax.experimental.pallas import tpu as pltpu
from jax.sharding import PartitionSpec as P

inner_coeff = 9.0 / 8.0
outer_coeff = -1.0 / 24.0
ratio = outer_coeff / inner_coeff
advance_time_step = 0.15
vmem_limit = 16 << 20

PX, PY, PZ, SXX, SYY, SXY, SXZ, SYZ = range(8)
ADJOINT = 8
BUOYANCY = 16
FIELDS = 17
STATE_SLOT = {SXX: 3, SYY: 4, SXY: 6, SXZ: 7, SYZ: 8}
ALONG_X = (SXX, SXY, SXZ)
SUB, LANE = 8, 128
RING = 24
SLOT = 6
SLOTS = 21


def row_slots(depth):
    three = [
        (base + field, z) for z in range(depth) for base in (0, ADJOINT) for field in ALONG_X
    ]
    two = [
        (field, z)
        for z in range(depth)
        for field in range(FIELDS)
        if field == BUOYANCY or field % ADJOINT not in ALONG_X
    ]
    slots, tile, sub = [], 0, 0
    while three or two:
        if three and sub <= 3:
            (field, z), rows = three.pop(0), 3
        else:
            (field, z), rows = two.pop(0), 2
        slots.append((field, z, rows, tile, sub))
        sub += rows
        if sub + 2 > SUB:
            tile, sub = tile + 1, 0
    return slots, tile + (sub > 0)


def column_slots(depth):
    return [(field, z) for z in range(depth) for field in range(FIELDS)]


def turn(value, amount, axis):
    amount %= value.shape[axis]
    return pltpu.roll(value, amount, axis) if amount else value


def sublanes():
    return lax.broadcasted_iota(jnp.int32, (SUB, LANE), 0)


def column_slot_of():
    return jnp.bitwise_and(lax.broadcasted_iota(jnp.int32, (SUB, LANE), 1) + 3, LANE - 1)


def even(axis):
    return jnp.bitwise_and(lax.axis_index(axis), 1) == 0


def pick(condition, first, second):
    return jnp.where(jnp.broadcast_to(condition, first.shape), first, second)


def lookup(mask_ref, element_ref, table_ref, z, row):
    element = element_ref[z, row : row + SUB, :]
    weight = mask_ref[z, row : row + SUB, :].astype(jnp.float32)
    lane = jnp.bitwise_and(element, LANE - 1)
    part = jnp.right_shift(element, 7)
    parts = table_ref.shape[2] // LANE
    found = []
    for first in range(3):
        value = None
        for k in range(parts):
            part_lanes = slice(LANE * k, LANE * (k + 1))
            entries = jnp.broadcast_to(table_ref[first, :, part_lanes], (SUB, LANE))
            taken = jnp.take_along_axis(entries, lane, axis=1, mode="promise_in_bounds")
            value = taken if k == 0 else jnp.where(part == k, taken, value)
        found.append(weight * value)
    return found


def pack_columns(load, depth, write):
    slot = column_slot_of()
    value = None
    slots = column_slots(depth)
    for k, (field, z) in enumerate(slots):
        tile, place = divmod(k, SLOTS)
        moved = turn(load(field, z), SLOT * place, 1)
        if place == 0:
            value = moved
        else:
            value = jnp.where(slot >= SLOT * place, moved, value)
        if place == SLOTS - 1 or k == len(slots) - 1:
            write(tile, value)


def depth_diff(plane, z, depth, offset):
    inside = lambda k: plane(k) if 0 <= k < depth else None

    def difference(high, low):
        if high is None:
            return None if low is None else -low
        return high if low is None else high - low

    near = difference(inside(z + 1 + offset), inside(z + offset))
    far = difference(inside(z + 2 + offset), inside(z - 1 + offset))
    return near if far is None else near + ratio * far


def own_tile(pushed_ref, forward_ref, adjoint_ref, buoyancy_ref, field, z, row):
    rows = slice(row, row + SUB)
    if field == BUOYANCY:
        return buoyancy_ref[z, rows, :]
    adjoint, field = divmod(field, ADJOINT)
    if field <= PZ:
        return pushed_ref[3 * adjoint + field, z, rows, :]
    return (adjoint_ref if adjoint else forward_ref)[0, STATE_SLOT[field], z, rows, :]


def first_pack(
    forward_hbm,
    adjoint_hbm,
    buoyancy_hbm,
    mask_hbm,
    element_hbm,
    table_hbm,
    first_ref,
    second_ref,
    pushed_ref,
    forward_ref,
    adjoint_ref,
    buoyancy_ref,
    mask_ref,
    element_ref,
    table_ref,
    arrivals,
):
    depth, rows, _ = buoyancy_ref.shape
    loads = [
        pltpu.make_async_copy(source, target, arrivals.at[k])
        for k, (source, target) in enumerate(
            (
                (element_hbm, element_ref),
                (mask_hbm, mask_ref),
                (table_hbm, table_ref),
                (buoyancy_hbm, buoyancy_ref),
                (forward_hbm, forward_ref),
                (adjoint_hbm, adjoint_ref),
            )
        )
    ]
    for copy in loads:
        copy.start()
    for copy in loads[:3]:
        copy.wait()
    cells = [(z, row) for z in range(depth) for row in range(0, rows, SUB)]
    for z, row in cells:
        for i, forcing in enumerate(lookup(mask_ref, element_ref, table_ref, z, row)):
            pushed_ref[i, z, row : row + SUB, :] = advance_time_step * forcing
    loads[3].wait()
    for state_ref, copy, base, step in (
        (forward_ref, loads[4], 0, advance_time_step),
        (adjoint_ref, loads[5], 3, -advance_time_step),
    ):
        copy.wait()
        for z, row in cells:
            part = slice(row, row + SUB)
            scaled = (step * inner_coeff) * buoyancy_ref[z, part, :]
            for i, (field, offset) in enumerate(((7, 0), (8, 0), (5, -1))):
                along = depth_diff(lambda k: state_ref[0, field, k, part, :], z, depth, offset)
                value = state_ref[0, i, z, part, :] + scaled * along
                if base == 0:
                    value = value + pushed_ref[i, z, part, :]
                pushed_ref[base + i, z, part, :] = value

    load = functools.partial(own_tile, pushed_ref, forward_ref, adjoint_ref, buoyancy_ref)
    slots, tiles = row_slots(depth)
    sub = sublanes()
    is_even = even("gx")
    for tile in range(tiles):
        up, down = None, None
        for field, z, count, at, start in slots:
            if at != tile:
                continue
            last = turn(load(field, z, rows - SUB), start + count, 0)
            first = turn(load(field, z, 0), start, 0)
            up = last if up is None else jnp.where(sub >= start, last, up)
            down = first if down is None else jnp.where(sub >= start, first, down)
        first_ref[tile] = pick(is_even, up, down)
        second_ref[tile] = pick(is_even, down, up)


def own_columns(pushed_ref, forward_ref, adjoint_ref, buoyancy_ref, columns_ref):
    depth, rows, _ = buoyancy_ref.shape
    load = functools.partial(own_tile, pushed_ref, forward_ref, adjoint_ref, buoyancy_ref)
    for row in range(0, rows, SUB):

        def write(tile, value, row=row):
            columns_ref[tile, row : row + SUB, :] = value

        pack_columns(lambda field, z, row=row: load(field, z, row), depth, write)


def second_pack(first_ref, second_ref, own_ref, columns_ref, rows_ref):
    depth = rows_ref.shape[1]
    slots, _ = row_slots(depth)
    is_even = even("gx")
    sub = sublanes()
    tiles = {}
    for field, z, count, tile, start in slots:
        if tile not in tiles:
            first, second = first_ref[tile], second_ref[tile]
            tiles[tile] = (pick(is_even, second, first), pick(is_even, first, second))
        up, down = tiles[tile]
        before = turn(up, SUB - count - start, 0)
        after = turn(down, -start, 0)
        rows_ref[field, z] = jnp.where(sub < 4, after, before)
    own = own_ref.shape[1]
    columns_ref[:, :own, :] = own_ref[...]

    def write(tile, value):
        columns_ref[tile, own:, :] = value

    pack_columns(lambda field, z: rows_ref[field, z], depth, write)


def ahead(value, axis):
    return (turn(value, -1, axis) - value) + ratio * (turn(value, -2, axis) - turn(value, 1, axis))


def behind(value, axis):
    return (value - turn(value, 1, axis)) + ratio * (turn(value, -1, axis) - turn(value, 2, axis))


def crossing(here, there):
    lane = lax.broadcasted_iota(jnp.int32, here.shape, 1)

    def at(k):
        if k == 0:
            return here
        return turn(jnp.where(lane < k if k > 0 else lane >= LANE + k, there, here), -k, 1)

    return at


def ahead_at(at):
    return (at(1) - at(0)) + ratio * (at(2) - at(-1))


def behind_at(at):
    return (at(0) - at(-1)) + ratio * (at(1) - at(-2))


def advance(
    forward_ref,
    adjoint_ref,
    pushed_ref,
    buoyancy_ref,
    rows_ref,
    first_ref,
    second_ref,
    terms_ref,
    moved_ref,
    rates_ref,
    field_ref,
    speed_ref,
):
    depth, rows, _ = buoyancy_ref.shape
    load = functools.partial(own_tile, pushed_ref, forward_ref, adjoint_ref, buoyancy_ref)
    slot = column_slot_of()
    from_next = slot >= SLOT * SLOTS
    for place in range(SLOTS):
        from_next = from_next | ((slot >= SLOT * place + 3) & (slot < SLOT * place + 6))
    from_first = from_next == jnp.broadcast_to(even("gy"), (SUB, LANE))
    merged = {}
    for k, (field, z) in enumerate(column_slots(depth)):
        tile, place = divmod(k, SLOTS)
        for row in range(0, RING, SUB):
            part = slice(row, row + SUB)
            field_ref[field, z, part, :LANE] = (
                load(field, z, row) if row < rows else rows_ref[field, z]
            )
            if (tile, row) not in merged:
                merged[tile, row] = jnp.where(
                    from_first, first_ref[tile, part, :], second_ref[tile, part, :]
                )
            field_ref[field, z, part, LANE:] = turn(merged[tile, row], -SLOT * place, 1)

    for state, step in ((0, advance_time_step), (1, -advance_time_step)):
        for z in range(depth):
            get = lambda field: field_ref[state * ADJOINT + field, z]
            scaled = (step * inner_coeff) * field_ref[BUOYANCY, z]
            sxy = get(SXY)
            changes = (
                behind(get(SXX), 0) + ahead(sxy, 1),
                ahead(sxy, 0) + behind(get(SYY), 1),
                ahead(get(SXZ), 0) + ahead(get(SYZ), 1),
            )
            for i, change in enumerate(changes):
                speed = get(i) + scaled * change
                speed_ref[3 * state + i, z, :, :LANE] = speed[:, :LANE]
                speed_ref[3 * state + i, z, :rows, LANE:] = speed[:rows, LANE:]

    for z in range(depth):
        rates = []
        for base in (0, 3):
            along = lambda i, offset: depth_diff(
                lambda k: speed_ref[base + i, k, :rows, :LANE], z, depth, offset
            )
            over_x = lambda i, way: way(speed_ref[base + i, z, :, :LANE], 0)[:rows]
            over_y = lambda i, way: way(
                crossing(
                    speed_ref[base + i, z, :rows, :LANE], speed_ref[base + i, z, :rows, LANE:]
                )
            )
            rates.append(
                (
                    over_x(0, ahead),
                    over_y(1, ahead_at),
                    along(2, 0),
                    over_y(0, behind_at) + over_x(1, behind),
                    along(0, -1) + over_x(2, behind),
                    along(1, -1) + over_y(2, behind_at),
                )
            )
        one, two = rates
        first_invariant = (one[0] + one[1] + one[2]) * (two[0] + two[1] + two[2])
        modulus = 2.0 * (one[0] * two[0] + one[1] * two[1] + one[2] * two[2])
        modulus = modulus + one[3] * two[3] + one[4] * two[4] + one[5] * two[5]
        density = None
        for i in range(3):
            moved = speed_ref[i, z, :rows, :LANE]
            moved_ref[i, z] = moved
            gain = moved * (speed_ref[3 + i, z, :rows, :LANE] - adjoint_ref[0, i, z])
            density = gain if density is None else density + gain
        for i in range(6):
            rates_ref[i, z] = one[i]
        terms_ref[0, z] = (inner_coeff * inner_coeff) * first_invariant
        terms_ref[1, z] = (inner_coeff * inner_coeff) * modulus
        terms_ref[2, z] = density / advance_time_step


def advance_stress(
    forward_ref, lame_ref, shear_ref, moved_ref, rates_ref, next_hbm, next_ref, leaves
):
    step = advance_time_step * inner_coeff
    for z in range(lame_ref.shape[0]):
        shear = step * shear_ref[z]
        dilatation = rates_ref[0, z] + rates_ref[1, z] + rates_ref[2, z]
        pressure = step * lame_ref[z] * dilatation
        for i in range(3):
            next_ref[0, i, z] = moved_ref[i, z]
            next_ref[0, 3 + i, z] = forward_ref[0, 3 + i, z] + (
                pressure + 2.0 * shear * rates_ref[i, z]
            )
            next_ref[0, 6 + i, z] = forward_ref[0, 6 + i, z] + shear * rates_ref[3 + i, z]
    copy = pltpu.make_async_copy(next_ref, next_hbm, leaves)
    copy.start()
    copy.wait()


def add_pair(one_ref, two_ref, _, sum_ref):
    total = one_ref[...] + two_ref[...]
    for copy in range(sum_ref.shape[0]):
        sum_ref[copy] = total


def on_chip(kernel, out_shapes, scratch=(), cost=0, far=(), away=()):
    vmem, anywhere = [pl.BlockSpec(memory_space=space) for space in (pltpu.VMEM, pl.ANY)]
    place = lambda k, value: pltpu.with_memory_space_constraint(
        value, pltpu.HBM if k in far else pltpu.VMEM
    )
    return lambda *operands: pl.pallas_call(
        kernel,
        out_shape=[
            (pltpu.HBM if k in away else pltpu.VMEM)(shape, jnp.float32)
            for k, shape in enumerate(out_shapes)
        ],
        in_specs=[anywhere if k in far else vmem for k in range(len(operands))],
        out_specs=[anywhere if k in away else vmem for k in range(len(out_shapes))],
        scratch_shapes=list(scratch),
        cost_estimate=pl.CostEstimate(flops=cost, bytes_accessed=cost, transcendentals=0),
        compiler_params=pltpu.CompilerParams(vmem_limit_bytes=vmem_limit),
    )(*[place(k, value) for k, value in enumerate(operands)])


def swaps(devices, start):
    pairs = [(i, i + 1) for i in range(start, devices - 1, 2)]
    return pairs + [(j, i) for i, j in pairs]


def exchange(first, second, axis):
    devices = lax.axis_size(axis)
    return (
        lax.ppermute(first, axis, swaps(devices, 0)),
        lax.ppermute(second, axis, swaps(devices, 1)),
    )


def shards(
    forward_state,
    adjoint_state,
    first_lame_parameter,
    shear_stiffness,
    buoyancy,
    layer_mask,
    layer_element,
    layer_forces,
):
    depth, rows, lanes = buoyancy.shape
    events = lax.axis_size("ev")
    table = jnp.transpose(layer_forces, (1, 0, 2))
    tiles = row_slots(depth)[1]
    column_tiles = -(-depth * FIELDS // SLOTS)
    message = (tiles, SUB, lanes)
    state, plane = forward_state.shape, buoyancy.shape
    first, second, pushed, forward_here, adjoint_here, buoyancy_here = on_chip(
        first_pack,
        [message, message, (6,) + plane, state, state, plane],
        [
            pltpu.VMEM(plane, jnp.int32),
            pltpu.VMEM(plane, jnp.int32),
            pltpu.VMEM(table.shape, jnp.float32),
            pltpu.SemaphoreType.DMA((6,)),
        ],
        cost=2_000_000,
        far=range(6),
    )(forward_state, adjoint_state, buoyancy, layer_mask, layer_element, table)
    first, second = exchange(first, second, "gx")
    (columns,) = on_chip(own_columns, [(column_tiles, rows, lanes)], cost=1_000_000)(
        pushed, forward_here, adjoint_here, buoyancy_here
    )
    columns, edge_rows = on_chip(
        second_pack,
        [(column_tiles, RING, lanes), (FIELDS, depth, SUB, lanes)],
        cost=1_000_000,
    )(first, second, columns)
    first, second = exchange(columns, columns, "gy")
    terms, moved, rates = on_chip(
        advance,
        [(3,) + plane, (3,) + plane, (6,) + plane],
        [
            pltpu.VMEM((FIELDS, depth, RING, 2 * lanes), jnp.float32),
            pltpu.VMEM((6, depth, RING, 2 * lanes), jnp.float32),
        ],
        cost=4_000_000,
    )(forward_here, adjoint_here, pushed, buoyancy_here, edge_rows, first, second)
    partner = lax.ppermute(terms, "ev", [(i, i ^ 1) for i in range(events)])
    (forward_next,) = on_chip(
        advance_stress,
        [state],
        [pltpu.VMEM(state, jnp.float32), pltpu.SemaphoreType.DMA(())],
        cost=2_000_000,
        away=(0,),
    )(
        forward_here, first_lame_parameter, shear_stiffness, moved, rates
    )
    (pairs,) = on_chip(add_pair, [(events // 2, 3) + plane], cost=500_000, far=(2,))(
        terms, partner, forward_next
    )
    groups = [list(range(k, events, 2)) for k in range(2)]
    kernels = jnp.sum(
        lax.all_to_all(pairs, "ev", 0, 0, axis_index_groups=groups, tiled=True), axis=0
    )
    return (forward_next, kernels)


def solution(mesh):
    in_specs = (
        P("ev", None, None, "gx", "gy"),
        P("ev", None, None, "gx", "gy"),
        P(None, "gx", "gy"),
        P(None, "gx", "gy"),
        P(None, "gx", "gy"),
        P(None, "gx", "gy"),
        P(None, "gx", "gy"),
        P("ev", None, None),
    )
    out_specs = (P("ev", None, None, "gx", "gy"), P(None, None, "gx", "gy"))
    return jax.shard_map(shards, mesh=mesh, in_specs=in_specs, out_specs=out_specs, check_vma=False)
```

```python
import functools

import jax
import jax.numpy as jnp
from jax import lax
from jax.experimental import pallas as pl
from jax.experimental.pallas import tpu as pltpu
from jax.sharding import PartitionSpec as P

inner_coeff = 9.0 / 8.0
outer_coeff = -1.0 / 24.0
ratio = outer_coeff / inner_coeff
advance_time_step = 0.15
vmem_limit = 16 << 20

PX, PY, PZ, SXX, SYY, SXY, SXZ, SYZ = range(8)
ADJOINT = 8
BUOYANCY = 16
FIELDS = 17
STATE_SLOT = {SXX: 3, SYY: 4, SXY: 6, SXZ: 7, SYZ: 8}
ALONG_X = (SXX, SXY, SXZ)
SUB, LANE = 8, 128
RING = 24
SLOT = 6
SLOTS = 21


def row_slots(depth):
    three = [
        (base + field, z) for z in range(depth) for base in (0, ADJOINT) for field in ALONG_X
    ]
    two = [
        (field, z)
        for z in range(depth)
        for field in range(FIELDS)
        if field == BUOYANCY or field % ADJOINT not in ALONG_X
    ]
    slots, tile, sub = [], 0, 0
    while three or two:
        if three and sub <= 3:
            (field, z), rows = three.pop(0), 3
        else:
            (field, z), rows = two.pop(0), 2
        slots.append((field, z, rows, tile, sub))
        sub += rows
        if sub + 2 > SUB:
            tile, sub = tile + 1, 0
    return slots, tile + (sub > 0)


def column_slots(depth):
    return [(field, z) for z in range(depth) for field in range(FIELDS)]


def turn(value, amount, axis):
    amount %= value.shape[axis]
    return pltpu.roll(value, amount, axis) if amount else value


def sublanes():
    return lax.broadcasted_iota(jnp.int32, (SUB, LANE), 0)


def column_slot_of():
    return jnp.bitwise_and(lax.broadcasted_iota(jnp.int32, (SUB, LANE), 1) + 3, LANE - 1)


def even(axis):
    return jnp.bitwise_and(lax.axis_index(axis), 1) == 0


def pick(condition, first, second):
    return jnp.where(jnp.broadcast_to(condition, first.shape), first, second)


def lookup(mask_ref, element_ref, table_ref, z, row):
    element = element_ref[z, row : row + SUB, :]
    weight = mask_ref[z, row : row + SUB, :].astype(jnp.float32)
    lane = jnp.bitwise_and(element, LANE - 1)
    part = jnp.right_shift(element, 7)
    parts = table_ref.shape[2] // LANE
    found = []
    for first in range(3):
        value = None
        for k in range(parts):
            part_lanes = slice(LANE * k, LANE * (k + 1))
            entries = jnp.broadcast_to(table_ref[first, :, part_lanes], (SUB, LANE))
            taken = jnp.take_along_axis(entries, lane, axis=1, mode="promise_in_bounds")
            value = taken if k == 0 else jnp.where(part == k, taken, value)
        found.append(weight * value)
    return found


def pack_columns(load, depth, write):
    slot = column_slot_of()
    value = None
    slots = column_slots(depth)
    for k, (field, z) in enumerate(slots):
        tile, place = divmod(k, SLOTS)
        moved = turn(load(field, z), SLOT * place, 1)
        if place == 0:
            value = moved
        else:
            value = jnp.where(slot >= SLOT * place, moved, value)
        if place == SLOTS - 1 or k == len(slots) - 1:
            write(tile, value)


def depth_diff(plane, z, depth, offset):
    inside = lambda k: plane(k) if 0 <= k < depth else None

    def difference(high, low):
        if high is None:
            return None if low is None else -low
        return high if low is None else high - low

    near = difference(inside(z + 1 + offset), inside(z + offset))
    far = difference(inside(z + 2 + offset), inside(z - 1 + offset))
    return near if far is None else near + ratio * far


def own_tile(pushed_ref, forward_ref, adjoint_ref, buoyancy_ref, field, z, row):
    rows = slice(row, row + SUB)
    if field == BUOYANCY:
        return buoyancy_ref[z, rows, :]
    adjoint, field = divmod(field, ADJOINT)
    if field <= PZ:
        return pushed_ref[3 * adjoint + field, z, rows, :]
    return (adjoint_ref if adjoint else forward_ref)[0, STATE_SLOT[field], z, rows, :]


def first_pack(
    forward_hbm,
    adjoint_hbm,
    buoyancy_hbm,
    mask_hbm,
    element_hbm,
    table_hbm,
    first_ref,
    second_ref,
    pushed_ref,
    forward_ref,
    adjoint_ref,
    buoyancy_ref,
    mask_ref,
    element_ref,
    table_ref,
    arrivals,
):
    depth, rows, _ = buoyancy_ref.shape
    loads = [
        pltpu.make_async_copy(source, target, arrivals.at[k])
        for k, (source, target) in enumerate(
            (
                (element_hbm, element_ref),
                (mask_hbm, mask_ref),
                (table_hbm, table_ref),
                (buoyancy_hbm, buoyancy_ref),
                (forward_hbm, forward_ref),
                (adjoint_hbm, adjoint_ref),
            )
        )
    ]
    for copy in loads:
        copy.start()
    for copy in loads[:3]:
        copy.wait()
    cells = [(z, row) for z in range(depth) for row in range(0, rows, SUB)]
    for z, row in cells:
        for i, forcing in enumerate(lookup(mask_ref, element_ref, table_ref, z, row)):
            pushed_ref[i, z, row : row + SUB, :] = advance_time_step * forcing
    loads[3].wait()
    for state_ref, copy, base, step in (
        (forward_ref, loads[4], 0, advance_time_step),
        (adjoint_ref, loads[5], 3, -advance_time_step),
    ):
        copy.wait()
        for z, row in cells:
            part = slice(row, row + SUB)
            scaled = (step * inner_coeff) * buoyancy_ref[z, part, :]
            for i, (field, offset) in enumerate(((7, 0), (8, 0), (5, -1))):
                along = depth_diff(lambda k: state_ref[0, field, k, part, :], z, depth, offset)
                value = state_ref[0, i, z, part, :] + scaled * along
                if base == 0:
                    value = value + pushed_ref[i, z, part, :]
                pushed_ref[base + i, z, part, :] = value

    load = functools.partial(own_tile, pushed_ref, forward_ref, adjoint_ref, buoyancy_ref)
    slots, tiles = row_slots(depth)
    sub = sublanes()
    is_even = even("gx")
    for tile in range(tiles):
        up, down = None, None
        for field, z, count, at, start in slots:
            if at != tile:
                continue
            last = turn(load(field, z, rows - SUB), start + count, 0)
            first = turn(load(field, z, 0), start, 0)
            up = last if up is None else jnp.where(sub >= start, last, up)
            down = first if down is None else jnp.where(sub >= start, first, down)
        first_ref[tile] = pick(is_even, up, down)
        second_ref[tile] = pick(is_even, down, up)


def own_columns(pushed_ref, forward_ref, adjoint_ref, buoyancy_ref, columns_ref):
    depth, rows, _ = buoyancy_ref.shape
    load = functools.partial(own_tile, pushed_ref, forward_ref, adjoint_ref, buoyancy_ref)
    for row in range(0, rows, SUB):

        def write(tile, value, row=row):
            columns_ref[tile, row : row + SUB, :] = value

        pack_columns(lambda field, z, row=row: load(field, z, row), depth, write)


def second_pack(first_ref, second_ref, own_ref, columns_ref, rows_ref):
    depth = rows_ref.shape[1]
    slots, _ = row_slots(depth)
    is_even = even("gx")
    sub = sublanes()
    tiles = {}
    for field, z, count, tile, start in slots:
        if tile not in tiles:
            first, second = first_ref[tile], second_ref[tile]
            tiles[tile] = (pick(is_even, second, first), pick(is_even, first, second))
        up, down = tiles[tile]
        before = turn(up, SUB - count - start, 0)
        after = turn(down, -start, 0)
        rows_ref[field, z] = jnp.where(sub < 4, after, before)
    own = own_ref.shape[1]
    columns_ref[:, :own, :] = own_ref[...]

    def write(tile, value):
        columns_ref[tile, own:, :] = value

    pack_columns(lambda field, z: rows_ref[field, z], depth, write)


def ahead(value, axis):
    return (turn(value, -1, axis) - value) + ratio * (turn(value, -2, axis) - turn(value, 1, axis))


def behind(value, axis):
    return (value - turn(value, 1, axis)) + ratio * (turn(value, -1, axis) - turn(value, 2, axis))


def crossing(here, there):
    lane = lax.broadcasted_iota(jnp.int32, here.shape, 1)

    def at(k):
        if k == 0:
            return here
        return turn(jnp.where(lane < k if k > 0 else lane >= LANE + k, there, here), -k, 1)

    return at


def ahead_at(at):
    return (at(1) - at(0)) + ratio * (at(2) - at(-1))


def behind_at(at):
    return (at(0) - at(-1)) + ratio * (at(1) - at(-2))


def advance(
    forward_ref,
    adjoint_ref,
    pushed_ref,
    buoyancy_ref,
    rows_ref,
    first_ref,
    second_ref,
    terms_ref,
    moved_ref,
    rates_ref,
    field_ref,
    speed_ref,
):
    depth, rows, _ = buoyancy_ref.shape
    load = functools.partial(own_tile, pushed_ref, forward_ref, adjoint_ref, buoyancy_ref)
    slot = column_slot_of()
    from_next = slot >= SLOT * SLOTS
    for place in range(SLOTS):
        from_next = from_next | ((slot >= SLOT * place + 3) & (slot < SLOT * place + 6))
    from_first = from_next == jnp.broadcast_to(even("gy"), (SUB, LANE))
    merged = {}
    for k, (field, z) in enumerate(column_slots(depth)):
        tile, place = divmod(k, SLOTS)
        for row in range(0, RING, SUB):
            part = slice(row, row + SUB)
            field_ref[field, z, part, :LANE] = (
                load(field, z, row) if row < rows else rows_ref[field, z]
            )
            if (tile, row) not in merged:
                merged[tile, row] = jnp.where(
                    from_first, first_ref[tile, part, :], second_ref[tile, part, :]
                )
            field_ref[field, z, part, LANE:] = turn(merged[tile, row], -SLOT * place, 1)

    for state, step in ((0, advance_time_step), (1, -advance_time_step)):
        for z in range(depth):
            get = lambda field: field_ref[state * ADJOINT + field, z]
            scaled = (step * inner_coeff) * field_ref[BUOYANCY, z]
            ways = ((SXX, behind, SXY, ahead), (SXY, ahead, SYY, behind), (SXZ, ahead, SYZ, ahead))
            for i, (tall, way_x, wide, way_y) in enumerate(ways):
                over_x = way_x(get(tall), 0)
                across, push = get(wide), get(i)
                over_y = way_y(across[:rows], 1)
                speed_ref[3 * state + i, z, :rows, :] = push[:rows] + scaled[:rows] * (
                    over_x[:rows] + over_y
                )
                edge_way = ahead_at if way_y is ahead else behind_at
                over_y = edge_way(crossing(across[rows:, :LANE], across[rows:, LANE:]))
                speed_ref[3 * state + i, z, rows:, :LANE] = push[rows:, :LANE] + scaled[
                    rows:, :LANE
                ] * (over_x[rows:, :LANE] + over_y)

    for z in range(depth):
        rates = []
        for base in (0, 3):
            along = lambda i, offset: depth_diff(
                lambda k: speed_ref[base + i, k, :rows, :LANE], z, depth, offset
            )
            over_x = lambda i, way: way(speed_ref[base + i, z, :, :LANE], 0)[:rows]
            over_y = lambda i, way: way(
                crossing(
                    speed_ref[base + i, z, :rows, :LANE], speed_ref[base + i, z, :rows, LANE:]
                )
            )
            rates.append(
                (
                    over_x(0, ahead),
                    over_y(1, ahead_at),
                    along(2, 0),
                    over_y(0, behind_at) + over_x(1, behind),
                    along(0, -1) + over_x(2, behind),
                    along(1, -1) + over_y(2, behind_at),
                )
            )
        one, two = rates
        first_invariant = (one[0] + one[1] + one[2]) * (two[0] + two[1] + two[2])
        modulus = 2.0 * (one[0] * two[0] + one[1] * two[1] + one[2] * two[2])
        modulus = modulus + one[3] * two[3] + one[4] * two[4] + one[5] * two[5]
        density = None
        for i in range(3):
            moved = speed_ref[i, z, :rows, :LANE]
            moved_ref[i, z] = moved
            gain = moved * (speed_ref[3 + i, z, :rows, :LANE] - adjoint_ref[0, i, z])
            density = gain if density is None else density + gain
        for i in range(6):
            rates_ref[i, z] = one[i]
        terms_ref[0, z] = (inner_coeff * inner_coeff) * first_invariant
        terms_ref[1, z] = (inner_coeff * inner_coeff) * modulus
        terms_ref[2, z] = density / advance_time_step


def advance_stress(
    forward_ref, lame_ref, shear_ref, moved_ref, rates_ref, next_hbm, next_ref, leaves
):
    step = advance_time_step * inner_coeff
    for z in range(lame_ref.shape[0]):
        shear = step * shear_ref[z]
        dilatation = rates_ref[0, z] + rates_ref[1, z] + rates_ref[2, z]
        pressure = step * lame_ref[z] * dilatation
        for i in range(3):
            next_ref[0, i, z] = moved_ref[i, z]
            next_ref[0, 3 + i, z] = forward_ref[0, 3 + i, z] + (
                pressure + 2.0 * shear * rates_ref[i, z]
            )
            next_ref[0, 6 + i, z] = forward_ref[0, 6 + i, z] + shear * rates_ref[3 + i, z]
    copy = pltpu.make_async_copy(next_ref, next_hbm, leaves)
    copy.start()
    copy.wait()


def add_pair(one_ref, two_ref, _, sum_ref):
    total = one_ref[...] + two_ref[...]
    for copy in range(sum_ref.shape[0]):
        sum_ref[copy] = total


def on_chip(kernel, out_shapes, scratch=(), cost=0, far=(), away=()):
    vmem, anywhere = [pl.BlockSpec(memory_space=space) for space in (pltpu.VMEM, pl.ANY)]
    place = lambda k, value: pltpu.with_memory_space_constraint(
        value, pltpu.HBM if k in far else pltpu.VMEM
    )
    return lambda *operands: pl.pallas_call(
        kernel,
        out_shape=[
            (pltpu.HBM if k in away else pltpu.VMEM)(shape, jnp.float32)
            for k, shape in enumerate(out_shapes)
        ],
        in_specs=[anywhere if k in far else vmem for k in range(len(operands))],
        out_specs=[anywhere if k in away else vmem for k in range(len(out_shapes))],
        scratch_shapes=list(scratch),
        cost_estimate=pl.CostEstimate(flops=cost, bytes_accessed=cost, transcendentals=0),
        compiler_params=pltpu.CompilerParams(vmem_limit_bytes=vmem_limit),
    )(*[place(k, value) for k, value in enumerate(operands)])


def swaps(devices, start):
    pairs = [(i, i + 1) for i in range(start, devices - 1, 2)]
    return pairs + [(j, i) for i, j in pairs]


def exchange(first, second, axis):
    devices = lax.axis_size(axis)
    return (
        lax.ppermute(first, axis, swaps(devices, 0)),
        lax.ppermute(second, axis, swaps(devices, 1)),
    )


def shards(
    forward_state,
    adjoint_state,
    first_lame_parameter,
    shear_stiffness,
    buoyancy,
    layer_mask,
    layer_element,
    layer_forces,
):
    depth, rows, lanes = buoyancy.shape
    events = lax.axis_size("ev")
    table = jnp.transpose(layer_forces, (1, 0, 2))
    tiles = row_slots(depth)[1]
    column_tiles = -(-depth * FIELDS // SLOTS)
    message = (tiles, SUB, lanes)
    state, plane = forward_state.shape, buoyancy.shape
    first, second, pushed, forward_here, adjoint_here, buoyancy_here = on_chip(
        first_pack,
        [message, message, (6,) + plane, state, state, plane],
        [
            pltpu.VMEM(plane, jnp.int32),
            pltpu.VMEM(plane, jnp.int32),
            pltpu.VMEM(table.shape, jnp.float32),
            pltpu.SemaphoreType.DMA((6,)),
        ],
        cost=2_000_000,
        far=range(6),
    )(forward_state, adjoint_state, buoyancy, layer_mask, layer_element, table)
    first, second = exchange(first, second, "gx")
    (columns,) = on_chip(own_columns, [(column_tiles, rows, lanes)], cost=1_000_000)(
        pushed, forward_here, adjoint_here, buoyancy_here
    )
    columns, edge_rows = on_chip(
        second_pack,
        [(column_tiles, RING, lanes), (FIELDS, depth, SUB, lanes)],
        cost=1_000_000,
    )(first, second, columns)
    first, second = exchange(columns, columns, "gy")
    terms, moved, rates = on_chip(
        advance,
        [(3,) + plane, (3,) + plane, (6,) + plane],
        [
            pltpu.VMEM((FIELDS, depth, RING, 2 * lanes), jnp.float32),
            pltpu.VMEM((6, depth, RING, 2 * lanes), jnp.float32),
        ],
        cost=4_000_000,
    )(forward_here, adjoint_here, pushed, buoyancy_here, edge_rows, first, second)
    partner = lax.ppermute(terms, "ev", [(i, i ^ 1) for i in range(events)])
    (forward_next,) = on_chip(
        advance_stress,
        [state],
        [pltpu.VMEM(state, jnp.float32), pltpu.SemaphoreType.DMA(())],
        cost=2_000_000,
        away=(0,),
    )(
        forward_here, first_lame_parameter, shear_stiffness, moved, rates
    )
    (pairs,) = on_chip(add_pair, [(events // 2, 3) + plane], cost=500_000, far=(2,))(
        terms, partner, forward_next
    )
    groups = [list(range(k, events, 2)) for k in range(2)]
    kernels = jnp.sum(
        lax.all_to_all(pairs, "ev", 0, 0, axis_index_groups=groups, tiled=True), axis=0
    )
    return (forward_next, kernels)


def solution(mesh):
    in_specs = (
        P("ev", None, None, "gx", "gy"),
        P("ev", None, None, "gx", "gy"),
        P(None, "gx", "gy"),
        P(None, "gx", "gy"),
        P(None, "gx", "gy"),
        P(None, "gx", "gy"),
        P(None, "gx", "gy"),
        P("ev", None, None),
    )
    out_specs = (P("ev", None, None, "gx", "gy"), P(None, None, "gx", "gy"))
    return jax.shard_map(shards, mesh=mesh, in_specs=in_specs, out_specs=out_specs, check_vma=False)
```
